32 devices in a mesh: dp: 8 (over y, x, core), tensor: 4 (over z).
Axes of the slice: x: 2, y: 2, z: 4, core: 2. Of those that a mesh axis runs over, the one named last changes fastest.
Arguments:
- grad_inproj: bfloat16 [8, 768, 2304], P('dp', None, 'tensor'), may hold values from -32 to 32
- error_inproj: float32 [8, 768, 2304], P('dp', None, 'tensor'), may hold values from -3 to 3
- basis_inproj: float32 [2304, 32], P('tensor'), may hold values from -6 to 6
- weight_inproj: float32 [768, 2304], P('dp', 'tensor'), may hold values from -0.3 to 0.3
- moment_inproj: float32 [768, 2304], P('dp', 'tensor'), may hold values from -0.3 to 0.3
- grad_outproj: bfloat16 [8, 768, 768], P('dp', 'tensor'), may hold values from -32 to 32
- error_outproj: float32 [8, 768, 768], P('dp', 'tensor'), may hold values from -3 to 3
- basis_outproj: float32 [768, 32], replicated, may hold values from -6 to 6
- weight_outproj: float32 [768, 768], P(('tensor', 'dp')), may hold values from -0.3 to 0.3
- moment_outproj: float32 [768, 768], P(('tensor', 'dp')), may hold values from -0.3 to 0.3
- grad_expand: bfloat16 [8, 768, 3072], P('dp', None, 'tensor'), may hold values from -32 to 32
- error_expand: float32 [8, 768, 3072], P('dp', None, 'tensor'), may hold values from -3 to 3
- basis_expand: float32 [3072, 32], P('tensor'), may hold values from -6 to 6
- weight_expand: float32 [768, 3072], P('dp', 'tensor'), may hold values from -0.3 to 0.3
- moment_expand: float32 [768, 3072], P('dp', 'tensor'), may hold values from -0.3 to 0.3
- grad_contract: bfloat16 [8, 3072, 768], P('dp', 'tensor'), may hold values from -32 to 32
- error_contract: float32 [8, 3072, 768], P('dp', 'tensor'), may hold values from -3 to 3
- basis_contract: float32 [768, 32], replicated, may hold values from -6 to 6
- weight_contract: float32 [3072, 768], P(('tensor', 'dp')), may hold values from -0.3 to 0.3
- moment_contract: float32 [3072, 768], P(('tensor', 'dp')), may hold values from -0.3 to 0.3
Outputs:
- residue_inproj: float32 [8, 768, 2304], P('dp', None, 'tensor')
- factor_inproj: float32 [2304, 32], P('tensor')
- master_inproj: float32 [768, 2304], P('dp', 'tensor')
- velocity_inproj: float32 [768, 2304], P('dp', 'tensor')
- serving_inproj: bfloat16 [768, 2304], P(None, 'tensor')
- residue_outproj: float32 [8, 768, 768], P('dp', 'tensor')
- factor_outproj: float32 [768, 32], replicated
- master_outproj: float32 [768, 768], P(('tensor', 'dp'))
- velocity_outproj: float32 [768, 768], P(('tensor', 'dp'))
- serving_outproj: bfloat16 [768, 768], P('tensor')
- residue_expand: float32 [8, 768, 3072], P('dp', None, 'tensor')
- factor_expand: float32 [3072, 32], P('tensor')
- master_expand: float32 [768, 3072], P('dp', 'tensor')
- velocity_expand: float32 [768, 3072], P('dp', 'tensor')
- serving_expand: bfloat16 [768, 3072], P(None, 'tensor')
- residue_contract: float32 [8, 3072, 768], P('dp', 'tensor')
- factor_contract: float32 [768, 32], replicated
- master_contract: float32 [3072, 768], P(('tensor', 'dp'))
- velocity_contract: float32 [3072, 768], P(('tensor', 'dp'))
- serving_contract: bfloat16 [3072, 768], P('tensor')
The draws below stay inside these ranges and needn't reach their ends.
All inputs are finite; a program needn't handle non-finite values.
Results may differ from the reference program's by a relative error of at most 0.012.
Values may be sent and summed in bfloat16 or wider, within the bound.
A program may use at most 128 MiB of HBM per device.

```python
import jax
import jax.numpy as jnp
from jax import lax

D = 768
FF = 3072
HEADS = 12
HEAD_DIM = 64
RANK = 32
NS_STEPS = 5
REPLICAS = 8


def gradient_draw(key, height, breadth):
    keys = jax.random.split(key, 3)
    row_factor = jnp.exp(jax.random.uniform(keys[1], (height,), jnp.float32, -0.8, 0.8))
    ramp = 1.0 + 2.0 * jnp.arange(height, dtype=jnp.float32) / (height - 1)
    col_factor = jnp.exp(jax.random.uniform(keys[2], (breadth,), jnp.float32, -0.8, 0.8))
    values = jnp.clip(jax.random.normal(keys[0], (REPLICAS, height, breadth), jnp.float32), -4.0, 4.0)
    scaled = 0.5 * values * (row_factor * ramp)[None, :, None] * col_factor[None, None, :]
    return scaled.astype(jnp.bfloat16)


def draw_grad_inproj(key, part):
    return gradient_draw(jax.random.fold_in(key, 11), D, 3 * HEADS * HEAD_DIM)


def draw_grad_outproj(key, part):
    return gradient_draw(jax.random.fold_in(key, 23), HEADS * HEAD_DIM, D)


def draw_grad_expand(key, part):
    return gradient_draw(jax.random.fold_in(key, 37), D, FF)


def draw_grad_contract(key, part):
    return gradient_draw(jax.random.fold_in(key, 41), FF, D)


def block_levels(key, shape, cuts, least, largest):
    factor_of, own = 1.0, jax.random.fold_in(key, 6)
    for dim, blocks in cuts:
        heights = jnp.exp(jax.random.uniform(jax.random.fold_in(own, dim), (blocks,), jnp.float32, least / len(cuts), largest / len(cuts)))
        factor_of = factor_of * jnp.repeat(heights, shape[dim] // blocks).reshape([-1 if axis == dim else 1 for axis in range(len(shape))])
    return factor_of


def normal_values(stream_key, dims, spread, most, cuts=(), kind=jnp.bfloat16):
    array = jax.random.normal(stream_key, dims, jnp.float32) * spread
    if len(cuts) > 0:
        array = block_levels(stream_key, dims, cuts, -0.22, 0.18) * array
    return jnp.clip(array, min=-most, max=most).astype(kind)


def setup_inputs(seed: int = 0) -> dict:
    key_of = jax.random.split(jax.random.key(seed), 21)
    return {
        "grad_inproj": draw_grad_inproj(jax.random.fold_in(key_of[20], 71), 0),
        "error_inproj": normal_values(key_of[1], (REPLICAS, D, 3 * HEADS * HEAD_DIM), 0.5, 3.0, ((0, 8), (2, 4)), jnp.float32),
        "basis_inproj": normal_values(key_of[2], (3 * HEADS * HEAD_DIM, RANK), 1.0, 6.0, ((0, 4),), jnp.float32),
        "weight_inproj": normal_values(key_of[3], (D, 3 * HEADS * HEAD_DIM), 0.05, 0.3, ((0, 8), (1, 4)), jnp.float32),
        "moment_inproj": normal_values(key_of[4], (D, 3 * HEADS * HEAD_DIM), 0.05, 0.3, ((0, 8), (1, 4)), jnp.float32),
        "grad_outproj": draw_grad_outproj(jax.random.fold_in(key_of[20], 71), 0),
        "error_outproj": normal_values(key_of[6], (REPLICAS, HEADS * HEAD_DIM, D), 0.5, 3.0, ((0, 8), (1, 4)), jnp.float32),
        "basis_outproj": normal_values(key_of[7], (D, RANK), 1.0, 6.0, (), jnp.float32),
        "weight_outproj": normal_values(key_of[8], (HEADS * HEAD_DIM, D), 0.05, 0.3, ((0, 32),), jnp.float32),
        "moment_outproj": normal_values(key_of[9], (HEADS * HEAD_DIM, D), 0.05, 0.3, ((0, 32),), jnp.float32),
        "grad_expand": draw_grad_expand(jax.random.fold_in(key_of[20], 71), 0),
        "error_expand": normal_values(key_of[11], (REPLICAS, D, FF), 0.5, 3.0, ((0, 8), (2, 4)), jnp.float32),
        "basis_expand": normal_values(key_of[12], (FF, RANK), 1.0, 6.0, ((0, 4),), jnp.float32),
        "weight_expand": normal_values(key_of[13], (D, FF), 0.05, 0.3, ((0, 8), (1, 4)), jnp.float32),
        "moment_expand": normal_values(key_of[14], (D, FF), 0.05, 0.3, ((0, 8), (1, 4)), jnp.float32),
        "grad_contract": draw_grad_contract(jax.random.fold_in(key_of[20], 71), 0),
        "error_contract": normal_values(key_of[16], (REPLICAS, FF, D), 0.5, 3.0, ((0, 8), (1, 4)), jnp.float32),
        "basis_contract": normal_values(key_of[17], (D, RANK), 1.0, 6.0, (), jnp.float32),
        "weight_contract": normal_values(key_of[18], (FF, D), 0.05, 0.3, ((0, 32),), jnp.float32),
        "moment_contract": normal_values(key_of[19], (FF, D), 0.05, 0.3, ((0, 32),), jnp.float32),
    }


momentum_beta = 0.9
step_size = 0.05

def matmul_high(left, right):
    return jnp.dot(left, right, precision=lax.Precision.HIGHEST, preferred_element_type=jnp.float32)

def inverse_root(gram):
    identity = jnp.eye(gram.shape[0], dtype=jnp.float32)
    norm_total = jnp.sqrt(jnp.sum(gram * gram)) + 1e-06
    iter_y = gram / norm_total
    iter_z = identity
    for repeat in range(NS_STEPS):
        middle = 1.5 * identity - 0.5 * matmul_high(iter_z, iter_y)
        iter_y = matmul_high(iter_y, middle)
        iter_z = matmul_high(middle, iter_z)
    return iter_z / jnp.sqrt(norm_total)

def compress(grad, error, basis, weight, moment):
    replicas = grad.shape[0]

    def left_term(index, total):
        merged = grad[index].astype(jnp.float32) + error[index]
        return total + matmul_high(merged, basis)
    left_sum = lax.fori_loop(0, replicas, left_term, jnp.zeros((grad.shape[1], basis.shape[1]), jnp.float32))
    left = left_sum / replicas
    gram = matmul_high(left.T, left)
    normed = matmul_high(left, inverse_root(gram))

    def right_term(index, total):
        merged = grad[index].astype(jnp.float32) + error[index]
        return total + matmul_high(merged.T, normed)
    right_sum = lax.fori_loop(0, replicas, right_term, jnp.zeros((grad.shape[2], basis.shape[1]), jnp.float32))
    factor = right_sum / replicas
    approx = matmul_high(normed, factor.T)
    residue = grad.astype(jnp.float32) + error - approx[None]
    velocity = momentum_beta * moment + approx
    master = weight - step_size * velocity
    return (residue, factor, master, velocity, master.astype(jnp.bfloat16))

def reference(grad_inproj, error_inproj, basis_inproj, weight_inproj, moment_inproj, grad_outproj, error_outproj, basis_outproj, weight_outproj, moment_outproj, grad_expand, error_expand, basis_expand, weight_expand, moment_expand, grad_contract, error_contract, basis_contract, weight_contract, moment_contract):
    first = compress(grad_inproj, error_inproj, basis_inproj, weight_inproj, moment_inproj)
    second = compress(grad_outproj, error_outproj, basis_outproj, weight_outproj, moment_outproj)
    third = compress(grad_expand, error_expand, basis_expand, weight_expand, moment_expand)
    fourth = compress(grad_contract, error_contract, basis_contract, weight_contract, moment_contract)
    return (first[0], first[1], first[2], first[3], first[4], second[0], second[1], second[2], second[3], second[4], third[0], third[1], third[2], third[3], third[4], fourth[0], fourth[1], fourth[2], fourth[3], fourth[4])
```

```python
import functools

import jax
import jax.numpy as jnp
from jax import lax
from jax.experimental import pallas as pl
from jax.experimental.pallas import tpu as pltpu
from jax.sharding import PartitionSpec as P

NS_STEPS = 5
RANK = 32
COUNT = 4
LANES = RANK * COUNT
COLS = 2 * RANK

momentum_beta = 0.9
step_size = 0.05

MESH = pl.DeviceIdType.MESH
F32 = jnp.float32
BF16 = jnp.bfloat16
HIGHEST = lax.Precision.HIGHEST


def dot_high(a, b, dims=(((1,), (0,)), ((), ()))):
    return lax.dot_general(a, b, dims, precision=HIGHEST, preferred_element_type=F32)


def lane_block(shape, dim):
    return lax.broadcasted_iota(jnp.int32, shape, dim) // RANK


def compact_gram(chunk):
    gram = dot_high(chunk, chunk, (((0,), (0,)), ((), ())))
    block = lane_block((RANK, LANES), 1)
    total = jnp.zeros((RANK, LANES), F32)
    for b in range(COUNT):
        total = total + jnp.where(block == b, gram[b * RANK:(b + 1) * RANK, :], 0.0)
    return total


def inverse_root(compact):
    same = lane_block((LANES, LANES), 0) == lane_block((LANES, LANES), 1)
    gram = jnp.where(same, jnp.concatenate([compact] * COUNT, axis=0), 0.0)
    identity = jnp.where(
        lax.broadcasted_iota(jnp.int32, (LANES, LANES), 0)
        == lax.broadcasted_iota(jnp.int32, (LANES, LANES), 1), 1.0, 0.0)
    squares = jnp.sum(compact * compact, axis=0, keepdims=True)
    block = lane_block((1, LANES), 1)
    norm = jnp.zeros((1, LANES), F32)
    for b in range(COUNT):
        part = jnp.sum(jnp.where(block == b, squares, 0.0), axis=1, keepdims=True)
        norm = jnp.where(block == b, part, norm)
    norm = jnp.sqrt(norm) + 1e-06
    iter_y = gram / norm
    iter_z = identity
    for repeat in range(NS_STEPS):
        zy = iter_y if repeat == 0 else dot_high(iter_z, iter_y)
        middle = 1.5 * identity - 0.5 * zy
        if repeat < NS_STEPS - 1:
            iter_y = dot_high(iter_y, middle)
        iter_z = middle if repeat == 0 else dot_high(middle, iter_z)
    return iter_z / jnp.sqrt(norm)


def split(x):
    hi = x.astype(BF16)
    return hi, (x - hi.astype(F32)).astype(BF16)


def factors_kernel(n, t, *refs):
    grads, errors, bases = refs[0:4], refs[4:8], refs[8:12]
    normed_ref, normed_out_ref, factor_ref = refs[12:15]
    gbuf, ebuf, merged, rhs = refs[15:19], refs[19:23], refs[23:27], refs[27]
    part, recv_part, cross, gathered = refs[28:32]
    fpart, recv_f, cross_f = refs[32:35]
    in_sem, s1, r1, s2, r2, s3, r3, s4, r4, s5, r5, s6, r6 = refs[35:48]

    me = lax.axis_index("dp")
    my_t = lax.axis_index("tensor")
    rows, width = part.shape[0], fpart.shape[1]
    h = rows // n
    rc = recv_f.shape[1]
    w = recv_f.shape[2]
    pieces = width // w

    loads = []
    for j in range(COUNT):
        pair = (
            pltpu.make_async_copy(grads[j].at[0], gbuf[j], in_sem.at[2 * j]),
            pltpu.make_async_copy(errors[j].at[0], ebuf[j], in_sem.at[2 * j + 1]),
        )
        for copy in pair:
            copy.start()
        loads.append(pair)

    barrier = pltpu.get_barrier_semaphore()
    for d in range(1, n):
        pl.semaphore_signal(barrier, inc=1, device_id={"dp": lax.rem(me + d, n)}, device_id_type=MESH)
    for d in range(1, t):
        pl.semaphore_signal(barrier, inc=1, device_id={"tensor": lax.rem(my_t + d, t)}, device_id_type=MESH)

    def exchange(axis, size, index, source, target, send, recv):
        out = []
        for d in range(1, size):
            peer = lax.rem(index + d, size)
            copy = pltpu.make_async_remote_copy(
                src_ref=source(peer), dst_ref=target(d), send_sem=send.at[d - 1], recv_sem=recv.at[d - 1],
                device_id={axis: peer}, device_id_type=MESH)
            copy.start()
            out.append(copy)
        return out

    def rows_of(peer):
        return pl.ds(pl.multiple_of(peer * h, 8), h)

    def piece_of(peer):
        if pieces == 1:
            return (pl.ds(pl.multiple_of(peer * rc, 8), rc), slice(None))
        return (pl.ds(pl.multiple_of((peer // pieces) * rc, 8), rc),
                pl.ds(pl.multiple_of(lax.rem(peer, pieces) * w, 128), w))

    part[...] = jnp.zeros_like(part)
    for j in range(COUNT):
        depth = bases[j].shape[0]
        columns = [jnp.zeros((depth, RANK), F32)] * COUNT
        columns[j] = bases[j][...]
        hi, lo = split(jnp.concatenate(columns, axis=1))
        rhs[0:depth, 0:LANES] = hi
        rhs[0:depth, LANES:2 * LANES] = lo
        for copy in loads[j]:
            copy.wait()
        height = gbuf[j].shape[0]
        step = min(height, 192)

        def block(i, carry, j=j, step=step, depth=depth):
            at = pl.ds(pl.multiple_of(i * step, 16), step)
            value = (gbuf[j][at, :].astype(F32) + ebuf[j][at, :]).astype(BF16)
            merged[j][at, :] = value
            both = jnp.dot(value, rhs[0:depth, :], preferred_element_type=F32)
            part[at, :] += both[:, :LANES] + both[:, LANES:]
            return carry

        lax.fori_loop(0, height // step, block, 0)

    pl.semaphore_wait(barrier, n - 1 + t - 1)

    first = exchange("dp", n, me, lambda p: part.at[rows_of(p), :], lambda d: recv_part.at[d - 1], s1, r1)
    chunk = part[rows_of(me), :]
    for d in range(1, n):
        first[d - 1].wait_recv()
        chunk = chunk + recv_part[d - 1]
    chunk = chunk / n
    cross[my_t, 0:h, :] = chunk
    cross[my_t, h:h + RANK, :] = compact_gram(chunk)
    second = exchange("tensor", t, my_t, lambda p: cross.at[my_t], lambda d: cross.at[my_t], s2, r2)
    for copy in second:
        copy.wait_recv()
    total = cross[0]
    for k in range(1, t):
        total = total + cross[k]
    col_lane = lax.broadcasted_iota(jnp.int32, (1, LANES), 1) < COLS
    mine = jnp.where(col_lane, total[0:h, :], chunk)
    gathered[me, 0:h, :] = mine
    gathered[me, h:h + RANK, :] = jnp.where(col_lane, compact_gram(mine), total[h:h + RANK, :])
    third = exchange("dp", n, me, lambda p: gathered.at[me], lambda d: gathered.at[me], s3, r3)
    for copy in third:
        copy.wait_recv()
    compact = gathered[0, h:h + RANK, :]
    for k in range(1, n):
        compact = compact + gathered[k, h:h + RANK, :]
    root = inverse_root(compact)
    left = gathered[:, 0:h, :].reshape(rows, LANES)
    normed = dot_high(left, root)
    hi, lo = split(normed)
    normed_ref[:, 0:LANES] = hi
    normed_ref[:, LANES:2 * LANES] = lo
    out_rows = normed_out_ref.shape[0]
    normed_out_ref[:, 0:LANES] = hi[0:out_rows]
    normed_out_ref[:, LANES:2 * LANES] = lo[0:out_rows]
    flipped_hi, flipped_lo = split(normed.T)

    fpart[...] = jnp.zeros_like(fpart)
    for j in range(COUNT):
        height, depth = merged[j].shape
        both = jnp.concatenate(
            [flipped_hi[j * RANK:(j + 1) * RANK, 0:height], flipped_lo[j * RANK:(j + 1) * RANK, 0:height]], axis=0)
        term = jnp.dot(both, merged[j][...], preferred_element_type=F32)
        fpart[j * RANK:(j + 1) * RANK, 0:depth] = term[0:RANK] + term[RANK:]

    fourth = exchange("dp", n, me, lambda p: fpart.at[piece_of(p)], lambda d: recv_f.at[d - 1], s4, r4)
    piece = fpart[piece_of(me)]
    for d in range(1, n):
        fourth[d - 1].wait_recv()
        piece = piece + recv_f[d - 1]
    piece = piece / n
    cross_f[my_t] = piece
    fifth = exchange("tensor", t, my_t, lambda p: cross_f.at[my_t], lambda d: cross_f.at[my_t], s5, r5)
    for copy in fifth:
        copy.wait_recv()
    total_f = cross_f[0]
    for k in range(1, t):
        total_f = total_f + cross_f[k]
    row_part = (me // pieces) * rc >= COLS
    factor_ref[piece_of(me)] = jnp.where(row_part, total_f, piece)
    sixth = exchange("dp", n, me, lambda p: factor_ref.at[piece_of(me)], lambda d: factor_ref.at[piece_of(me)], s6, r6)
    for copy in sixth:
        copy.wait_recv()
    for group in (first, second, third, fourth, fifth, sixth):
        for copy in group:
            copy.wait_send()


def factors(n, t, grads, errors, bases):
    rows = max(g.shape[1] for g in grads)
    width = max(g.shape[2] for g in grads)
    h = rows // n
    rc = max(8, LANES // n)
    pieces = n * rc // LANES
    w = width // pieces
    out_rows = grads[2].shape[1]
    dma = pltpu.SemaphoreType.DMA
    scratch = [pltpu.VMEM(g.shape[1:], BF16) for g in grads]
    scratch += [pltpu.VMEM(g.shape[1:], F32) for g in grads]
    scratch += [pltpu.VMEM(g.shape[1:], BF16) for g in grads]
    scratch += [
        pltpu.VMEM((width, 2 * LANES), BF16),
        pltpu.VMEM((rows, LANES), F32),
        pltpu.VMEM((n - 1, h, LANES), F32),
        pltpu.VMEM((t, h + RANK, LANES), F32),
        pltpu.VMEM((n, h + RANK, LANES), F32),
        pltpu.VMEM((LANES, width), F32),
        pltpu.VMEM((n - 1, rc, w), F32),
        pltpu.VMEM((t, rc, w), F32),
        dma((2 * COUNT,)),
    ]
    for size in (n, t, n, n, t, n):
        scratch += [dma((size - 1,)), dma((size - 1,))]
    return pl.pallas_call(
        functools.partial(factors_kernel, n, t),
        out_shape=(
            jax.ShapeDtypeStruct((rows, 2 * LANES), BF16),
            jax.ShapeDtypeStruct((out_rows, 2 * LANES), BF16),
            jax.ShapeDtypeStruct((LANES, width), F32),
        ),
        in_specs=[pl.BlockSpec(memory_space=pl.ANY)] * 8 + [pl.BlockSpec(memory_space=pltpu.VMEM)] * 4,
        out_specs=[pl.BlockSpec(memory_space=pltpu.VMEM)] * 3,
        scratch_shapes=scratch,
        compiler_params=pltpu.CompilerParams(
            collective_id=0, has_side_effects=True, vmem_limit_bytes=40 * 1024 * 1024),
        cost_estimate=pl.CostEstimate(flops=4_000_000_000, bytes_accessed=60_000_000, transcendentals=0),
        name="factors",
    )(*grads, *errors, *bases)


def update_kernel(*refs):
    normed, normed_out, factor = refs[0:3]
    ins, outs, rhs = refs[3:23], refs[23:39], refs[39]
    i = pl.program_id(0)
    me = lax.axis_index("dp")

    @pl.when(i == 0)
    def _():
        value = factor[...].astype(BF16)
        block = lane_block(value.shape, 0)
        for j in range(COUNT):
            masked = jnp.where(block == j, value, jnp.zeros_like(value))
            rhs[j, 0:LANES, :] = masked
            rhs[j, LANES:2 * LANES, :] = masked

    for j in range(COUNT):
        grad, error, weight, moment, early = ins[5 * j:5 * j + 5]
        residue, master, velocity, serving = outs[4 * j:4 * j + 4]
        width = grad.shape[2]
        lhs = normed_out[0] if j == 2 else normed[0]
        approx = jnp.dot(lhs, rhs[j, :, 0:width], preferred_element_type=F32)
        residue[0] = grad[0].astype(F32) + error[0] - approx
        serving[0] = (early[0].astype(F32) - step_size * approx).astype(BF16)

        @pl.when(i == me)
        def _(weight=weight, moment=moment, master=master, velocity=velocity, approx=approx):
            value = momentum_beta * moment[...] + approx
            velocity[...] = value
            master[...] = weight[...] - step_size * value


def update(n, normed, normed_out, factor, groups):
    def blocked(x, width=None):
        x = x.reshape(n, -1, x.shape[-1])
        return x, pl.BlockSpec((1,) + x.shape[1:], lambda i: (i, 0, 0))

    def whole(shape):
        return pl.BlockSpec(shape, lambda i: (0, 0))

    args, specs, out_shapes, out_specs = [], [], [], []
    for x in (normed, normed_out):
        x, spec = blocked(x)
        args.append(x)
        specs.append(spec)
    args.append(factor)
    specs.append(whole(factor.shape))
    for grad, error, weight, moment, early in groups:
        shapes = []
        for x in (grad, error):
            x, spec = blocked(x)
            args.append(x)
            specs.append(spec)
        blocks = x.shape
        args += [weight, moment]
        specs += [whole(weight.shape)] * 2
        x, spec = blocked(early)
        args.append(x)
        specs.append(spec)
        out_shapes += [jax.ShapeDtypeStruct(blocks, F32), jax.ShapeDtypeStruct(weight.shape, F32),
                       jax.ShapeDtypeStruct(weight.shape, F32), jax.ShapeDtypeStruct(blocks, BF16)]
        out_specs += [spec, whole(weight.shape), whole(weight.shape), spec]
    return pl.pallas_call(
        update_kernel,
        grid=(n,),
        out_shape=out_shapes,
        in_specs=specs,
        out_specs=out_specs,
        scratch_shapes=[pltpu.VMEM((COUNT, 2 * LANES, factor.shape[1]), BF16)],
        compiler_params=pltpu.CompilerParams(vmem_limit_bytes=40 * 1024 * 1024),
        name="update",
    )(*args)


def body(n, t, *args):
    inproj, outproj, expand, contract = (args[5 * k:5 * k + 5] for k in range(COUNT))
    order = (inproj, expand, outproj, contract)
    early = [
        lax.all_gather((w - step_size * momentum_beta * m).astype(BF16), "dp", axis=0, tiled=False)
        for _, _, _, w, m in order
    ]
    normed, normed_out, factor = factors(
        n, t, [g[0] for g in order], [g[1] for g in order], [g[2] for g in order])
    results = update(n, normed, normed_out, factor,
                     [(g[0], g[1], g[3], g[4], u) for g, u in zip(order, early)])
    outs = []
    for j in (0, 2, 1, 3):
        grad = order[j][0]
        height, width = grad.shape[1:]
        residue, master, velocity, serving = results[4 * j:4 * j + 4]
        outs += [residue.reshape(grad.shape), factor[j * RANK:(j + 1) * RANK, 0:width].T,
                 master, velocity, serving.reshape(height, width)]
    return tuple(outs)


def solution(mesh):
    col = (P("dp", None, "tensor"), P("dp", None, "tensor"), P("tensor", None), P("dp", "tensor"), P("dp", "tensor"))
    row = (P("dp", "tensor", None), P("dp", "tensor", None), P(), P(("tensor", "dp"), None), P(("tensor", "dp"), None))
    col_out = (P("dp", None, "tensor"), P("tensor", None), P("dp", "tensor"), P("dp", "tensor"), P(None, "tensor"))
    row_out = (P("dp", "tensor", None), P(), P(("tensor", "dp"), None), P(("tensor", "dp"), None), P("tensor", None))
    return jax.shard_map(
        functools.partial(body, mesh.shape["dp"], mesh.shape["tensor"]), mesh=mesh,
        in_specs=col + row + col + row, out_specs=col_out + row_out + col_out + row_out, check_vma=False)
```

```python
import functools

import jax
import jax.numpy as jnp
from jax import lax
from jax.experimental import pallas as pl
from jax.experimental.pallas import tpu as pltpu
from jax.sharding import PartitionSpec as P

NS_STEPS = 5
RANK = 32
COUNT = 4
LANES = RANK * COUNT
COLS = 2 * RANK

momentum_beta = 0.9
step_size = 0.05

MESH = pl.DeviceIdType.MESH
F32 = jnp.float32
BF16 = jnp.bfloat16
HIGHEST = lax.Precision.HIGHEST
VMEM_BYTES = 60 * 1024 * 1024


def dot_high(a, b, dims=(((1,), (0,)), ((), ()))):
    return lax.dot_general(a, b, dims, precision=HIGHEST, preferred_element_type=F32)


def lane_block(shape, dim):
    return lax.broadcasted_iota(jnp.int32, shape, dim) // RANK


def compact_gram(chunk):
    gram = dot_high(chunk, chunk, (((0,), (0,)), ((), ())))
    block = lane_block((RANK, LANES), 1)
    total = jnp.zeros((RANK, LANES), F32)
    for b in range(COUNT):
        total = total + jnp.where(block == b, gram[b * RANK:(b + 1) * RANK, :], 0.0)
    return total


def inverse_root(compact):
    same = lane_block((LANES, LANES), 0) == lane_block((LANES, LANES), 1)
    gram = jnp.where(same, jnp.concatenate([compact] * COUNT, axis=0), 0.0)
    identity = jnp.where(
        lax.broadcasted_iota(jnp.int32, (LANES, LANES), 0)
        == lax.broadcasted_iota(jnp.int32, (LANES, LANES), 1), 1.0, 0.0)
    squares = jnp.sum(compact * compact, axis=0, keepdims=True)
    block = lane_block((1, LANES), 1)
    norm = jnp.zeros((1, LANES), F32)
    for b in range(COUNT):
        part = jnp.sum(jnp.where(block == b, squares, 0.0), axis=1, keepdims=True)
        norm = jnp.where(block == b, part, norm)
    norm = jnp.sqrt(norm) + 1e-06
    iter_y = gram / norm
    iter_z = identity
    for repeat in range(NS_STEPS):
        zy = iter_y if repeat == 0 else dot_high(iter_z, iter_y)
        middle = 1.5 * identity - 0.5 * zy
        if repeat < NS_STEPS - 1:
            iter_y = dot_high(iter_y, middle)
        iter_z = middle if repeat == 0 else dot_high(middle, iter_z)
    return iter_z / jnp.sqrt(norm)


def split(x):
    hi = x.astype(BF16)
    return hi, (x - hi.astype(F32)).astype(BF16)


def factors_kernel(n, t, *refs):
    refs = list(refs)

    def take(count):
        out = refs[:count]
        del refs[:count]
        return out

    grads, errors, bases, weights, moments = (take(COUNT) for _ in range(5))
    normed_ref, normed_out_ref, flipped_ref, factor_ref, early_in_ref = take(5)
    early_refs = [None] + take(COUNT - 1)
    gbuf, ebuf, bbuf, wbuf, mbuf, own, merged = (take(COUNT) for _ in range(7))
    early_in, rhs, part, recv_part, cross, gathered, fpart, recv_f, cross_f, full_f = take(10)
    in_sem, w_sem, a_send, a_recv, f_send, f_recv = take(6)
    s1, r1, s2, r2, s3, r3, s4, r4, s5, r5, s6, r6 = take(12)
    early_refs[0] = early_in

    me = lax.axis_index("dp")
    my_t = lax.axis_index("tensor")
    rows, width = part.shape[0], fpart.shape[1]
    h = rows // n
    rc = recv_f.shape[1]
    w = recv_f.shape[2]
    pieces = width // w

    loads, late = [], []
    for j in range(COUNT):
        group = (
            pltpu.make_async_copy(bases[j], bbuf[j], in_sem.at[j, 0]),
            pltpu.make_async_copy(grads[j].at[0], gbuf[j], in_sem.at[j, 1]),
            pltpu.make_async_copy(errors[j].at[0], ebuf[j], in_sem.at[j, 2]),
        )
        for copy in group:
            copy.start()
        loads.append(group)
    for j in range(COUNT):
        group = (
            pltpu.make_async_copy(weights[j], wbuf[j], w_sem.at[j, 0]),
            pltpu.make_async_copy(moments[j], mbuf[j], w_sem.at[j, 1]),
        )
        for copy in group:
            copy.start()
        late.append(group)

    barrier = pltpu.get_barrier_semaphore()
    for d in range(1, n):
        pl.semaphore_signal(barrier, inc=1, device_id={"dp": lax.rem(me + d, n)}, device_id_type=MESH)
    for d in range(1, t):
        pl.semaphore_signal(barrier, inc=1, device_id={"tensor": lax.rem(my_t + d, t)}, device_id_type=MESH)

    def remote(axis, peer, source, target, send, recv):
        copy = pltpu.make_async_remote_copy(
            src_ref=source, dst_ref=target, send_sem=send, recv_sem=recv,
            device_id={axis: peer}, device_id_type=MESH)
        copy.start()
        return copy

    def exchange(axis, size, index, source, target, send, recv):
        out = []
        for d in range(1, size):
            peer = lax.rem(index + d, size)
            out.append(remote(axis, peer, source(peer), target(d), send.at[d - 1], recv.at[d - 1]))
        return out

    chips = n // 2
    sibling = me + 1 - 2 * lax.rem(me, 2)

    def early_start(j):
        for copy in late[j]:
            copy.wait()
        own[j][...] = (wbuf[j][...] - (step_size * momentum_beta) * mbuf[j][...]).astype(BF16)
        keep = pltpu.make_async_copy(own[j], early_refs[j].at[me], w_sem.at[j, 2])
        keep.start()
        out = [remote("dp", sibling, own[j], early_refs[j].at[me], a_send.at[j, 0], a_recv.at[j, 0])]
        for d in range(1, chips):
            out.append(remote("dp", lax.rem(me + 2 * d, n), own[j], early_refs[j].at[me],
                              a_send.at[j, d], a_recv.at[j, d]))
        return keep, out

    def early_forward(j, copies):
        out = []
        for d in range(1, chips):
            copies[d].wait_recv()
            origin = early_refs[j].at[lax.rem(me - 2 * d + n, n)]
            out.append(remote("dp", sibling, origin, origin, f_send.at[j, d - 1], f_recv.at[j, d - 1]))
        return out

    def rows_of(peer):
        return pl.ds(pl.multiple_of(peer * h, 8), h)

    def piece_of(peer):
        if pieces == 1:
            return (pl.ds(pl.multiple_of(peer * rc, 8), rc), slice(None))
        return (pl.ds(pl.multiple_of((peer // pieces) * rc, 8), rc),
                pl.ds(pl.multiple_of(lax.rem(peer, pieces) * w, 128), w))

    for copy in loads[0]:
        copy.wait()
    merged[0][...] = (gbuf[0][...].astype(F32) + ebuf[0][...]).astype(BF16)
    both = jnp.dot(jnp.concatenate(split(bbuf[0][...]), axis=0), merged[0][...], preferred_element_type=F32)
    term = both[0:RANK] + both[RANK:]
    part[...] = jnp.concatenate([term, jnp.zeros((LANES - RANK, rows), F32)], axis=0).T
    for j in range(1, COUNT):
        depth = bases[j].shape[1]
        for copy in loads[j]:
            copy.wait()
        columns = [jnp.zeros((RANK, depth), F32)] * COUNT
        columns[j] = bbuf[j][...]
        hi, lo = split(jnp.concatenate(columns, axis=0).T)
        rhs[0:depth, 0:LANES] = hi
        rhs[0:depth, LANES:2 * LANES] = lo
        height = gbuf[j].shape[0]
        step = min(height, 192)

        def block(i, carry, j=j, step=step, depth=depth):
            at = pl.ds(pl.multiple_of(i * step, 16), step)
            value = (gbuf[j][at, :].astype(F32) + ebuf[j][at, :]).astype(BF16)
            merged[j][at, :] = value
            both = jnp.dot(value, rhs[0:depth, :], preferred_element_type=F32)
            part[at, :] += both[:, :LANES] + both[:, LANES:]
            return carry

        lax.fori_loop(0, height // step, block, 0)

    pl.semaphore_wait(barrier, n - 1 + t - 1)

    first = exchange("dp", n, me, lambda p: part.at[rows_of(p), :], lambda d: recv_part.at[d - 1], s1, r1)
    keeps, sent, forwarded = {}, {}, {}
    keeps[0], sent[0] = early_start(0)
    chunk = part[rows_of(me), :]
    for d in range(1, n):
        first[d - 1].wait_recv()
        chunk = chunk + recv_part[d - 1]
    chunk = chunk / n
    cross[my_t, 0:h, :] = chunk
    cross[my_t, h:h + RANK, :] = compact_gram(chunk)
    second = exchange("tensor", t, my_t, lambda p: cross.at[my_t], lambda d: cross.at[my_t], s2, r2)
    for copy in second:
        copy.wait_recv()
    total = cross[0]
    for k in range(1, t):
        total = total + cross[k]
    col_lane = lax.broadcasted_iota(jnp.int32, (1, LANES), 1) < COLS
    mine = jnp.where(col_lane, total[0:h, :], chunk)
    gathered[me, 0:h, :] = mine
    gathered[me, h:h + RANK, :] = jnp.where(col_lane, compact_gram(mine), total[h:h + RANK, :])
    third = exchange("dp", n, me, lambda p: gathered.at[me], lambda d: gathered.at[me], s3, r3)
    for copy in third:
        copy.wait_recv()
    for j in range(1, COUNT):
        keeps[j], sent[j] = early_start(j)
    forwarded[0] = early_forward(0, sent[0])
    compact = gathered[0, h:h + RANK, :]
    for k in range(1, n):
        compact = compact + gathered[k, h:h + RANK, :]
    root = inverse_root(compact)
    left = gathered[:, 0:h, :].reshape(rows, LANES)
    normed = dot_high(left, root)
    hi, lo = split(normed)
    normed_ref[:, 0:LANES] = hi
    normed_ref[:, LANES:2 * LANES] = lo
    out_rows = normed_out_ref.shape[0]
    normed_out_ref[:, 0:LANES] = hi[0:out_rows]
    normed_out_ref[:, LANES:2 * LANES] = lo[0:out_rows]
    flipped_hi, flipped_lo = split(normed.T)
    flipped_ref[0:LANES, :] = flipped_hi
    flipped_ref[LANES:2 * LANES, :] = flipped_lo

    both = jnp.dot(merged[0][...], jnp.concatenate([hi, lo], axis=1), preferred_element_type=F32)
    depth = merged[0].shape[0]
    fpart[...] = jnp.zeros_like(fpart)
    fpart[0:RANK, 0:depth] = (both[:, :LANES] + both[:, LANES:]).T[0:RANK]
    for j in range(1, COUNT):
        height, depth = merged[j].shape
        both = jnp.concatenate(
            [flipped_hi[j * RANK:(j + 1) * RANK, 0:height], flipped_lo[j * RANK:(j + 1) * RANK, 0:height]], axis=0)
        term = jnp.dot(both, merged[j][...], preferred_element_type=F32)
        fpart[j * RANK:(j + 1) * RANK, 0:depth] = term[0:RANK] + term[RANK:]

    fourth = exchange("dp", n, me, lambda p: fpart.at[piece_of(p)], lambda d: recv_f.at[d - 1], s4, r4)
    piece = fpart[piece_of(me)]
    for d in range(1, n):
        fourth[d - 1].wait_recv()
        piece = piece + recv_f[d - 1]
    piece = piece / n
    cross_f[my_t] = piece
    fifth = exchange("tensor", t, my_t, lambda p: cross_f.at[my_t], lambda d: cross_f.at[my_t], s5, r5)
    for copy in fifth:
        copy.wait_recv()
    total_f = cross_f[0]
    for k in range(1, t):
        total_f = total_f + cross_f[k]
    row_part = (me // pieces) * rc >= COLS
    full_f[piece_of(me)] = jnp.where(row_part, total_f, piece)
    sixth = exchange("dp", n, me, lambda p: full_f.at[piece_of(me)], lambda d: full_f.at[piece_of(me)], s6, r6)
    for j in range(1, COUNT):
        forwarded[j] = early_forward(j, sent[j])
    keeps[0].wait()
    sent[0][0].wait_recv()
    for copy in forwarded[0]:
        copy.wait_recv()
    early_in_ref[...] = early_in[...].astype(F32).reshape(rows, early_in.shape[2]).T.astype(BF16)
    for copy in sixth:
        copy.wait_recv()
    factor_ref[...] = full_f[...]
    for j in range(1, COUNT):
        keeps[j].wait()
        sent[j][0].wait_recv()
        for copy in forwarded[j]:
            copy.wait_recv()
    groups = [first, second, third, fourth, fifth, sixth]
    groups += [sent[j] for j in range(COUNT)] + [forwarded[j] for j in range(COUNT)]
    for group in groups:
        for copy in group:
            copy.wait_send()


def factors(n, t, grads, errors, bases, weights, moments):
    rows = max(g.shape[1] for g in grads[1:])
    width = max(g.shape[2] for g in grads[1:])
    h = rows // n
    rc = max(8, LANES // n)
    pieces = n * rc // LANES
    w = width // pieces
    out_rows = grads[2].shape[1]
    dma = pltpu.SemaphoreType.DMA
    own = [x.shape for x in weights]
    early = [(n,) + shape for shape in own]
    scratch = [pltpu.VMEM(g.shape[1:], BF16) for g in grads]
    scratch += [pltpu.VMEM(g.shape[1:], F32) for g in grads]
    scratch += [pltpu.VMEM(g.shape, F32) for g in bases]
    scratch += [pltpu.VMEM(shape, F32) for shape in own + own]
    scratch += [pltpu.VMEM(shape, BF16) for shape in own]
    scratch += [pltpu.VMEM(g.shape[1:], BF16) for g in grads]
    scratch += [
        pltpu.VMEM(early[0], BF16),
        pltpu.VMEM((width, 2 * LANES), BF16),
        pltpu.VMEM((rows, LANES), F32),
        pltpu.VMEM((n - 1, h, LANES), F32),
        pltpu.VMEM((t, h + RANK, LANES), F32),
        pltpu.VMEM((n, h + RANK, LANES), F32),
        pltpu.VMEM((LANES, width), F32),
        pltpu.VMEM((n - 1, rc, w), F32),
        pltpu.VMEM((t, rc, w), F32),
        pltpu.VMEM((LANES, width), F32),
        dma((COUNT, 3)), dma((COUNT, 3)),
        dma((COUNT, n // 2)), dma((COUNT, n // 2)),
        dma((COUNT, n // 2 - 1)), dma((COUNT, n // 2 - 1)),
    ]
    for size in (n, t, n, n, t, n):
        scratch += [dma((size - 1,)), dma((size - 1,))]
    anywhere = pl.BlockSpec(memory_space=pl.ANY)
    return pl.pallas_call(
        functools.partial(factors_kernel, n, t),
        out_shape=[
            jax.ShapeDtypeStruct((rows, 2 * LANES), BF16),
            jax.ShapeDtypeStruct((out_rows, 2 * LANES), BF16),
            jax.ShapeDtypeStruct((2 * LANES, rows), BF16),
            jax.ShapeDtypeStruct((LANES, width), F32),
            jax.ShapeDtypeStruct((own[0][1], rows), BF16),
        ] + [jax.ShapeDtypeStruct(shape, BF16) for shape in early[1:]],
        in_specs=[anywhere] * (5 * COUNT),
        out_specs=[pl.BlockSpec()] * 5 + [anywhere] * (COUNT - 1),
        scratch_shapes=scratch,
        compiler_params=pltpu.CompilerParams(
            collective_id=0, has_side_effects=True, vmem_limit_bytes=VMEM_BYTES),
        cost_estimate=pl.CostEstimate(flops=4_000_000_000, bytes_accessed=60_000_000, transcendentals=0),
        name="factors",
    )(*grads, *errors, *bases, *weights, *moments)


def update_kernel(*refs):
    normed, normed_out, flipped, factor = refs[0:4]
    ins, outs, rhs, lhs_in = refs[4:24], refs[24:40], refs[40], refs[41]
    i = pl.program_id(0)
    me = lax.axis_index("dp")

    @pl.when(i == 0)
    def _():
        value = factor[...].astype(BF16)
        block = lane_block(value.shape, 0)
        for j in range(COUNT):
            masked = jnp.where(block == j, value, jnp.zeros_like(value))
            rhs[j, 0:LANES, :] = masked
            rhs[j, LANES:2 * LANES, :] = masked
        depth = lhs_in.shape[0] * lhs_in.shape[1]
        turned = factor[:, 0:depth].T
        turned = jnp.where(lane_block(turned.shape, 1) == 0, turned, 0.0)
        turned = turned.reshape(lhs_in.shape[0], lhs_in.shape[1], LANES).astype(BF16)
        lhs_in[:, :, 0:LANES] = turned
        lhs_in[:, :, LANES:2 * LANES] = turned

    for j in range(COUNT):
        grad, error, weight, moment, early = ins[5 * j:5 * j + 5]
        residue, master, velocity, serving = outs[4 * j:4 * j + 4]
        lhs = normed_out[0] if j == 2 else normed[0]
        factor_j = rhs.at[j, :, pl.ds(0, weight.shape[1])]
        if j == 0:
            approx = jnp.dot(lhs_in[i], flipped[...], preferred_element_type=F32)
        else:
            approx = jnp.dot(lhs, factor_j[...], preferred_element_type=F32)
        residue[0] = grad[0].astype(F32) + error[0] - approx
        serving[0] = (early[0].astype(F32) - step_size * approx).astype(BF16)

        @pl.when(i == me)
        def _(j=j, weight=weight, moment=moment, master=master, velocity=velocity, approx=approx,
              lhs=lhs, factor_j=factor_j):
            if j == 0:
                approx = jnp.dot(lhs, factor_j[...], preferred_element_type=F32)
            value = momentum_beta * moment[...] + approx
            velocity[...] = value
            master[...] = weight[...] - step_size * value


def update(n, normed, normed_out, flipped, factor, groups):
    def blocked(x):
        x = x.reshape(n, -1, x.shape[-1])
        return x, pl.BlockSpec((1,) + x.shape[1:], lambda i: (i, 0, 0))

    def whole(shape):
        return pl.BlockSpec(shape, lambda i: (0, 0))

    args, specs, out_shapes, out_specs = [], [], [], []
    for x in (normed, normed_out):
        x, spec = blocked(x)
        args.append(x)
        specs.append(spec)
    for x in (flipped, factor):
        args.append(x)
        specs.append(whole(x.shape))
    for grad, error, weight, moment, early in groups:
        for x in (grad, error):
            x, spec = blocked(x)
            args.append(x)
            specs.append(spec)
        blocks = x.shape
        args += [weight, moment]
        specs += [whole(weight.shape)] * 2
        x, spec = blocked(early)
        args.append(x)
        specs.append(spec)
        out_shapes += [jax.ShapeDtypeStruct(blocks, F32), jax.ShapeDtypeStruct(weight.shape, F32),
                       jax.ShapeDtypeStruct(weight.shape, F32), jax.ShapeDtypeStruct(blocks, BF16)]
        out_specs += [spec, whole(weight.shape), whole(weight.shape), spec]
    depth = groups[0][0].shape[1]
    return pl.pallas_call(
        update_kernel,
        grid=(n,),
        out_shape=out_shapes,
        in_specs=specs,
        out_specs=out_specs,
        scratch_shapes=[pltpu.VMEM((COUNT, 2 * LANES, factor.shape[1]), BF16),
                        pltpu.VMEM((n, depth // n, 2 * LANES), BF16)],
        compiler_params=pltpu.CompilerParams(vmem_limit_bytes=VMEM_BYTES),
        name="update",
    )(*args)


def body(n, t, *args):
    inproj, outproj, expand, contract = (args[5 * k:5 * k + 5] for k in range(COUNT))
    order = [list(inproj), list(expand), list(outproj), list(contract)]
    for k in (0, 1):
        order[0][k] = order[0][k].transpose(0, 2, 1)
    grads, errors, bases, weights, moments = (list(x) for x in zip(*order))
    outputs = factors(n, t, grads, errors, [x.T for x in bases], weights, moments)
    normed, normed_out, flipped, factor = outputs[0:4]
    early = outputs[4:]
    results = update(n, normed, normed_out, flipped, factor, list(zip(grads, errors, weights, moments, early)))
    outs = []
    for j in (0, 2, 1, 3):
        grad = grads[j]
        height, width = grad.shape[1:]
        residue, master, velocity, serving = results[4 * j:4 * j + 4]
        residue, serving = residue.reshape(grad.shape), serving.reshape(height, width)
        if j == 0:
            residue, serving = residue.transpose(0, 2, 1), serving.T
        outs += [residue, factor[j * RANK:(j + 1) * RANK, 0:master.shape[1]].T, master, velocity, serving]
    return tuple(outs)


def solution(mesh):
    col = (P("dp", None, "tensor"), P("dp", None, "tensor"), P("tensor", None), P("dp", "tensor"), P("dp", "tensor"))
    row = (P("dp", "tensor", None), P("dp", "tensor", None), P(), P(("tensor", "dp"), None), P(("tensor", "dp"), None))
    col_out = (P("dp", None, "tensor"), P("tensor", None), P("dp", "tensor"), P("dp", "tensor"), P(None, "tensor"))
    row_out = (P("dp", "tensor", None), P(), P(("tensor", "dp"), None), P(("tensor", "dp"), None), P("tensor", None))
    return jax.shard_map(
        functools.partial(body, mesh.shape["dp"], mesh.shape["tensor"]), mesh=mesh,
        in_specs=col + row + col + row, out_specs=col_out + row_out + col_out + row_out, check_vma=False)
```
